32 devices in a mesh: dp: 4 (over y, x), depth: 4 (over z), grid: 2 (over core).
Axes of the slice: x: 2, y: 2, z: 4, core: 2. Of those that a mesh axis runs over, the one named last changes fastest.
Arguments:
- tokens: bfloat16 [1024, 12288], P(('dp', 'depth'), 'grid'), may hold values from -6 to 6
- weight: bfloat16 [12288, 24576], P('grid', 'depth'), may hold values from -0.0546875 to 0.0546875
- cotangent: bfloat16 [1024, 24576], P(('dp', 'grid'), 'depth'), may hold values from -0.5 to 0.5
Outputs:
- hidden: bfloat16 [1024, 24576], P(('dp', 'grid'), 'depth')
- weight_grad: bfloat16 [12288, 24576], P(('grid', 'dp'), 'depth')
The draws below stay inside these ranges and needn't reach their ends.
All inputs are finite; a program needn't handle non-finite values.
Results may differ from the reference program's by a relative error of at most 0.011.
Values may be sent and summed in bfloat16 or wider, within the bound.
No kernel may reach another device: no remote copies, remote signals or barrier semaphores. Data moves between devices by JAX's collectives and lax.ppermute only.
A program may use at most 192 MiB of HBM per device.

```python
import jax
import jax.numpy as jnp

D = 12288
FF = 24576
TOKENS = 1024


def level_of(key, dims, split, least, largest):
    def one(axis_at, shards_of):
        draws = jax.random.uniform(jax.random.fold_in(jax.random.fold_in(key, 6), axis_at), (shards_of,), jnp.float32, least / len(split), largest / len(split))
        return jnp.repeat(jnp.exp(draws), dims[axis_at] // shards_of).reshape((-1,) + (1,) * (len(dims) - axis_at - 1))

    loudness = one(*split[0])
    for cut in split[1:]:
        loudness = loudness * one(*cut)
    return loudness


def noise(own_key, shape, width, reach, split=(), kind=jnp.bfloat16):
    gain = level_of(own_key, shape, split, -0.22, 0.18) if split else 1.0
    result = jax.random.normal(own_key, shape, jnp.float32) * width * gain
    return jnp.minimum(jnp.maximum(result, -reach), reach).astype(kind)


def setup_inputs(seed: int = 0) -> dict:
    splits = jax.random.split(jax.random.key(seed), 4)
    tokens = noise(splits[0], (TOKENS, D), 1.0, 6.0, ((0, 16), (1, 2)))
    weight = noise(splits[1], (D, FF), D ** -0.5, 0.0546875, ((0, 2), (1, 4)))
    cotangent = noise(splits[2], (TOKENS, FF), (TOKENS ** -0.5), 0.5, ((0, 8), (1, 4)))
    return {"tokens": tokens, "weight": weight, "cotangent": cotangent}


def gelu_tanh(values):
    return jax.nn.gelu(values, approximate=True)

def reference(tokens, weight, cotangent):
    preact = jnp.dot(tokens, weight, preferred_element_type=jnp.float32)
    activated, pullback = jax.vjp(gelu_tanh, preact)
    grad_pre = pullback(cotangent.astype(jnp.float32))[0].astype(jnp.bfloat16)
    weight_grad = jnp.dot(tokens.T, grad_pre, preferred_element_type=jnp.float32)
    return (activated.astype(jnp.bfloat16), weight_grad.astype(jnp.bfloat16))
```

```python
import functools

import jax
import jax.numpy as jnp
from jax import lax
from jax.experimental import pallas as pl
from jax.experimental.pallas import tpu as pltpu
from jax.sharding import PartitionSpec as P

F32, BF16 = jnp.float32, jnp.bfloat16
CHUNKS = 4
LIMIT = 60 << 20


def gelu_tanh(values):
    return jax.nn.gelu(values, approximate=True)


def swap(values, axis, bits):
    return lax.ppermute(values, axis, [(i, i ^ bits) for i in range(lax.axis_size(axis))])


def divisor(size, most):
    return next(n for n in range(min(size, most), 0, -1) if size % n == 0 and (n % 128 == 0 or n == size))


def forward_kernel(rows, half, where_ref, x0, e1, o1, e2, o2, e3, w_ref, *rest):
    *outs, lines, total, sems = rest
    n, k = pl.program_id(0), pl.program_id(1)
    depth, side = where_ref[1], where_ref[2]
    low = depth < 2
    end = (depth == 0) | (depth == 3)
    third, fourth = jnp.where(low, 2, 1), jnp.where(low, 3, 0)

    def put(source, place, slot):
        return pltpu.make_async_copy(source, lines.at[pl.ds(pl.multiple_of(place * rows, rows), rows), :], sems.at[slot])

    @pl.when((n == 0) & (k == 0))
    def _():
        put(x0, depth, 0).start()
        put(e1, depth ^ 1, 1).start()

        @pl.when(end)
        def _():
            put(e2, third, 2).start()
            put(e3, fourth, 3).start()

        @pl.when(jnp.logical_not(end))
        def _():
            put(o1, third, 2).start()
            put(o2, fourth, 3).start()

        put(x0, depth, 0).wait()
        put(e1, depth ^ 1, 1).wait()
        put(e2, third, 2).wait()
        put(e3, fourth, 3).wait()

    bk = w_ref.shape[0]
    part = jnp.dot(lines[:, pl.ds(pl.multiple_of(k * bk, bk), bk)], w_ref[...], preferred_element_type=F32)
    last = pl.num_programs(1) - 1

    @pl.when(k == 0)
    def _():
        total[...] = part

    @pl.when(k > 0)
    def _():
        total[...] += part

    @pl.when(k == last)
    def _():
        if len(outs) == 1:
            outs[0][...] = total[...]
            return
        keep, send = outs

        @pl.when(side == 0)
        def _():
            keep[...] = total[:half, :]
            send[...] = total[half:, :].astype(BF16)

        @pl.when(side != 0)
        def _():
            keep[...] = total[half:, :]
            send[...] = total[:half, :].astype(BF16)


def forward(where, pieces, weight, chunk, width, pair):
    rows, feats = pieces[0].shape
    every = 4 * rows
    half = every // 2
    bn, bk = divisor(width, 768), divisor(feats, 1536)
    if pair:
        outs = [jax.ShapeDtypeStruct((half, width), F32), jax.ShapeDtypeStruct((half, width), BF16)]
    else:
        outs = [jax.ShapeDtypeStruct((every, width), F32)]
    first = chunk * (width // bn)
    return pl.pallas_call(
        functools.partial(forward_kernel, rows, half),
        grid_spec=pltpu.PrefetchScalarGridSpec(
            num_scalar_prefetch=1,
            grid=(width // bn, feats // bk),
            in_specs=[pl.BlockSpec(memory_space=pl.ANY)] * 6 + [pl.BlockSpec((bk, bn), lambda n, k, s: (k, first + n))],
            out_specs=[pl.BlockSpec((o.shape[0], bn), lambda n, k, s: (0, n)) for o in outs],
            scratch_shapes=[
                pltpu.VMEM((every, feats), BF16),
                pltpu.VMEM((every, bn), F32),
                pltpu.SemaphoreType.DMA((4,)),
            ],
        ),
        out_shape=outs,
        compiler_params=pltpu.CompilerParams(vmem_limit_bytes=LIMIT),
        cost_estimate=pl.CostEstimate(
            flops=2 * every * feats * width, bytes_accessed=2 * feats * width + 2 * every * feats, transcendentals=0
        ),
        name="fwd%d" % chunk,
    )(where, *pieces, weight)


def grad_kernel(chunk, rows, part, spots, pairs, steps, where_ref, *refs):
    count = 16 + len(spots)
    tokens, grads = refs[:16], refs[16:count]
    out, left, right, made, left_sems, right_sems, out_sems = refs[-7:]
    dp, depth, side = where_ref[0], where_ref[1], where_ref[2]
    low = depth < 2
    places = (depth, depth ^ 1, jnp.where(low, 2, 1), jnp.where(low, 3, 0))
    bn = made.shape[2]
    width = right.shape[1]

    loads = []
    for s in range(4):
        for r in range(4):
            at = pl.multiple_of(((dp ^ s) * 4 + places[r]) * rows, rows)
            loads.append(pltpu.make_async_copy(tokens[4 * s + r], left.at[pl.ds(at, rows), :], left_sems.at[4 * s + r]))
    feeds = []
    for n in range(steps):
        feeds.append([])
        for i, (s, other) in enumerate(spots):
            at = pl.multiple_of(((dp ^ s) * pairs + (jnp.abs(other - side) if pairs == 2 else 0)) * part, part)
            feeds[n].append(
                pltpu.make_async_copy(
                    grads[i].at[:, pl.ds(n * bn, bn)],
                    right.at[pl.ds(at, part), pl.ds(n * bn, bn)],
                    right_sems.at[n * len(spots) + i],
                )
            )
    for copy in loads:
        copy.start()
    for step in feeds:
        for copy in step:
            copy.start()
    for copy in loads:
        copy.wait()
    stores = []
    for n in range(steps):
        for copy in feeds[n]:
            copy.wait()
        if n >= 2:
            stores[n - 2].wait()
        made[n % 2] = lax.dot_general(
            left[...], right[:, n * bn : (n + 1) * bn], (((0,), (0,)), ((), ())), preferred_element_type=F32
        ).astype(BF16)
        stores.append(
            pltpu.make_async_copy(made.at[n % 2], out.at[:, pl.ds(chunk * width + n * bn, bn)], out_sems.at[n % 2])
        )
        stores[n].start()
    for copy in stores[-2:]:
        copy.wait()


def weight_grad_block(where, tokens, grads, spots, so_far, chunk, hidden_units, pairs):
    rows, sub = tokens[0].shape
    part, width = grads[0].shape
    every = 16 * rows
    bn = divisor(width, 512)
    steps = width // bn
    given = [] if so_far is None else [so_far]
    return pl.pallas_call(
        functools.partial(grad_kernel, chunk, rows, part, spots, pairs, steps),
        in_specs=[pl.BlockSpec(memory_space=pltpu.SMEM)]
        + [pl.BlockSpec(memory_space=pl.ANY)] * (16 + len(grads) + len(given)),
        out_specs=pl.BlockSpec(memory_space=pl.ANY),
        out_shape=jax.ShapeDtypeStruct((sub, hidden_units), BF16),
        scratch_shapes=[
            pltpu.VMEM((every, sub), BF16),
            pltpu.VMEM((every, width), BF16),
            pltpu.VMEM((2, sub, bn), BF16),
            pltpu.SemaphoreType.DMA((16,)),
            pltpu.SemaphoreType.DMA((steps * len(grads),)),
            pltpu.SemaphoreType.DMA((2,)),
        ],
        input_output_aliases={17 + len(grads): 0} if given else {},
        compiler_params=pltpu.CompilerParams(vmem_limit_bytes=LIMIT),
        cost_estimate=pl.CostEstimate(
            flops=2 * every * sub * width,
            bytes_accessed=2 * (every * sub + every * width + sub * width),
            transcendentals=0,
        ),
        name="bwd%d" % chunk,
    )(where, *tokens, *grads, *given)


def local(tokens, weight, cotangent):
    pair = lax.axis_size("grid") == 2
    dp, depth, side = (lax.axis_index(a) for a in ("dp", "depth", "grid"))
    where = jnp.stack([dp, depth, side]).astype(jnp.int32)
    hidden_units = weight.shape[1]
    sub = tokens.shape[1] // 4
    width = hidden_units // CHUNKS

    e1 = swap(tokens, "depth", 1)
    o1 = lax.ppermute(tokens, "depth", [(1, 2), (2, 1)])
    e2 = lax.ppermute(o1, "depth", [(1, 0), (2, 3)])
    o2 = lax.ppermute(e1, "depth", [(1, 2), (2, 1)])
    e3 = lax.ppermute(o2, "depth", [(1, 0), (2, 3)])
    end = (depth == 0) | (depth == 3)
    blocks = (tokens, e1, jnp.where(end, e2, o1), jnp.where(end, e3, o2))

    def columns(block, s):
        cut = lax.dynamic_slice_in_dim(block, (dp ^ s) * sub, sub, 1)
        return swap(cut, "dp", s) if s else cut

    lefts = [[columns(b, s) for b in blocks] for s in range(4)]
    lefts = [b for group in lefts for b in group]

    hidden, grad = [], None
    for j in range(CHUNKS):
        made = forward(where, (tokens, e1, o1, e2, o2, e3), weight, j, width, pair)
        if pair:
            preact = made[0] + swap(made[1], "grid", 1).astype(F32)
        else:
            preact = lax.psum_scatter(made[0], "grid", scatter_dimension=0, tiled=True)
        activated, pullback = jax.vjp(gelu_tanh, preact)
        hidden.append(activated.astype(BF16))
        cot = lax.slice_in_dim(cotangent, j * width, (j + 1) * width, axis=1)
        own = pullback(cot.astype(F32))[0].astype(BF16)
        if not pair:
            own = lax.all_gather(own, "grid", axis=0, tiled=True)
        a, b = swap(own, "dp", 1), swap(own, "dp", 2)
        c = swap(b, "dp", 1) if j % 2 == 0 else swap(a, "dp", 2)
        grads, spots = [own, a, b, c], [(0, 0), (1, 0), (2, 0), (3, 0)]
        if pair:
            grads += [swap(v, "grid", 1) for v in grads]
            spots += [(s, 1) for s, _ in spots]
        grad = weight_grad_block(where, lefts, grads, tuple(spots), grad, j, hidden_units, 2 if pair else 1)
    return (jnp.concatenate(hidden, axis=1), grad)


def solution(mesh):
    assert mesh.shape["dp"] == 4 and mesh.shape["depth"] == 4
    return jax.shard_map(
        local,
        mesh=mesh,
        in_specs=(P(("dp", "depth"), "grid"), P("grid", "depth"), P(("dp", "grid"), "depth")),
        out_specs=(P(("dp", "grid"), "depth"), P(("grid", "dp"), "depth")),
        check_vma=False,
    )
```
